128 devices in a mesh: pb: 128 (over z, x, y, core).
Axes of the slice: x: 4, y: 4, z: 4, core: 2. Of those that a mesh axis runs over, the one named last changes fastest.
Arguments:
- densities: bfloat16 [128, 128, 32, 1200], P(None, 'pb'), may hold values from -1.1953125 to 1.1953125
- screening: bfloat16 [128, 1200, 1200], P('pb'), may hold values from -0.1875 to 0.1875
- live: int32 [128, 128], P(None, 'pb'), may hold values 0 or 1
Outputs:
- kernel: bfloat16 [128, 128, 256], P(None, 'pb')
The draws below stay inside these ranges and needn't reach their ends.
All inputs are finite; a program needn't handle non-finite values. No bound on the sum of `live` on one device may be relied on, other than what follows from the above.
Results may differ from the reference program's by a relative error of at most 0.0049.
Values may be sent and summed in bfloat16 or wider, within the bound.
A program may use at most 128 MiB of HBM per device.

```python
import jax
import jax.numpy as jnp
from jax import lax

NG = 1200
PAIRS = 16
KROWS = 128
QS = 128


def plant(result, rng, smallest, high):
    place = [jax.random.randint(jax.random.fold_in(rng, axis), (), 0, length) for axis, length in enumerate(result.shape)]
    widest = result.shape.index(max(result.shape))
    next_to = place[:widest] + [(place[widest] + 1) % result.shape[widest]] + place[widest + 1:]
    return result.at[tuple(place)].set(smallest).at[tuple(next_to)].set(high)


def steps_of(key, dims, split, least, high):
    loudness = 1.0
    for position, parts in split:
        heights = jax.random.uniform(jax.random.fold_in(jax.random.fold_in(key, 6), position), (parts,), jnp.float32, least / len(split), high / len(split))
        loudness = loudness * jnp.repeat(jnp.exp(heights), dims[position] // parts).reshape((-1,) + (1,) * (len(dims) - 1 - position))
    return loudness


def gaussian(own_key, shape, deviation, most, pieces=(), held_as=jnp.bfloat16):
    gain = steps_of(own_key, shape, pieces, -0.22, 0.18) if pieces else 1.0
    array = jax.random.normal(own_key, shape, jnp.float32) * deviation * gain
    return jnp.minimum(jnp.maximum(array, -most), most).astype(held_as)


def setup_inputs(seed: int = 0) -> dict:
    keys = jax.random.split(jax.random.key(seed), 4)
    return {
        "densities": gaussian(keys[0], (QS, KROWS, 2 * PAIRS, NG), 0.2, 1.1953125, ((1, 128),)),
        "screening": gaussian(keys[1], (QS, NG, NG), NG ** -0.5, 0.1875, ((0, 128),)),
        "live": plant((jax.random.randint(keys[2], (QS, KROWS), 0, 4) < 3).astype(jnp.int32), jax.random.fold_in(keys[2], 1), 0, 1),
    }


def one_q(args):
    rho, weights, mask = args
    pairs = rho.shape[1] // 2
    valence = rho[:, pairs:, :].reshape(-1, rho.shape[2])
    screened = jnp.dot(valence, weights.T, preferred_element_type=jnp.float32).astype(jnp.bfloat16)
    screened = screened.reshape(rho.shape[0], pairs, rho.shape[2])
    blocks = jnp.einsum("kag,kbg->kab", rho[:, :pairs, :].astype(jnp.float32), screened.astype(jnp.float32))
    blocks = blocks.reshape(rho.shape[0], pairs * pairs) * mask.astype(jnp.float32)[:, None]
    return blocks.astype(jnp.bfloat16)


def reference(densities, screening, live):
    return lax.map(one_q, (densities, screening, live))
```

```python
import jax
import jax.numpy as jnp
from jax import lax
from jax.experimental import pallas as pl
from jax.experimental.pallas import tpu as pltpu
from jax.sharding import PartitionSpec as P

F32 = jnp.float32
BF16 = jnp.bfloat16
MESH = pl.DeviceIdType.MESH

DEV = 128
PAIRS = 16
NG = 1200
MAIN = 1152
TAIL = NG - MAIN
HALF = 64
LANES_A = MAIN + 128
LANES_B = MAIN
STEP = 59
GROUP = 16
GROUPS = DEV // GROUP
PARTS_A = ((0, 384), (384, LANES_A))


def digits(i):
    return lax.div(i, 32), lax.rem(lax.div(i, 8), 4), lax.rem(lax.div(i, 2), 4), lax.rem(i, 2)


def undigits(z, x, y, c):
    return ((z * 4 + x) * 4 + y) * 2 + c


def target(me, slot):
    z, x, y, c = digits(me)
    dz, dx, dy, dc = digits(lax.rem(slot * STEP, DEV))
    return undigits(lax.rem(z + dz, 4), lax.rem(x + dx, 4), lax.rem(y + dy, 4), lax.rem(c + dc, 2))


def origin(me, slot):
    z, x, y, c = digits(me)
    dz, dx, dy, dc = digits(lax.rem(slot * STEP, DEV))
    return undigits(
        lax.rem(z + 4 - dz, 4), lax.rem(x + 4 - dx, 4), lax.rem(y + 4 - dy, 4), lax.rem(c + 2 - dc, 2)
    )


def same_block(shape, div0, mod0, div1, mod1):
    row = lax.broadcasted_iota(jnp.int32, shape, 0)
    col = lax.broadcasted_iota(jnp.int32, shape, 1)
    row = row // div0 if div0 > 1 else row % mod0
    col = col // div1 if div1 > 1 else col % mod1
    return row == col


def kernel(
    x_hbm, w_hbm, o_ref,
    xin, w_in, w_wide, send_a, send_b, recv_a, recv_b, screened, turn, spread, staged, landed,
    load_sem, send_sem, recv_sem_a, recv_sem_b, back_send_sem, back_recv_sem,
):
    me = lax.axis_index("pb")

    loads = [
        pltpu.make_async_copy(x_hbm.at[pl.ds(16, 16), pl.ds(0, 384)], xin.at[pl.ds(16, 16), pl.ds(0, 384)], load_sem.at[0]),
        pltpu.make_async_copy(x_hbm.at[pl.ds(16, 16), pl.ds(384, 816)], xin.at[pl.ds(16, 16), pl.ds(384, 816)], load_sem.at[1]),
        pltpu.make_async_copy(x_hbm.at[pl.ds(0, 16), pl.ds(MAIN, TAIL)], xin.at[pl.ds(0, 16), pl.ds(MAIN, TAIL)], load_sem.at[2]),
        pltpu.make_async_copy(x_hbm.at[pl.ds(0, 16), pl.ds(0, MAIN)], xin.at[pl.ds(0, 16), pl.ds(0, MAIN)], load_sem.at[3]),
        pltpu.make_async_copy(w_hbm, w_in, load_sem.at[4]),
    ]
    for load in loads:
        load.start()

    barrier = pltpu.get_barrier_semaphore()

    def greet(slot, _):
        pl.semaphore_signal(barrier, inc=1, device_id=(target(me, slot),), device_id_type=MESH)
        return 0

    lax.fori_loop(1, DEV, greet, 0)

    def turned(block):
        return jnp.transpose(block).astype(F32)

    def turn_block(first_row, column, slot, out, out_column):
        for r in range(PAIRS):
            turn[slot, :, r, :] = turned(xin[first_row + r, pl.ds(column, 128), :])
        out[:, :, pl.ds(out_column, 128)] = turn[slot].astype(BF16)

    def turn_blocks(first_row, begin, end, out):
        def body(j, _):
            column = pl.multiple_of(j * 128, 128)
            turn_block(first_row, column, lax.rem(j, 2), out, column)
            return 0

        lax.fori_loop(begin, end, body, 0)

    def send_part(src, dst, begin, width, sem_s, sem_r):
        def body(slot, _):
            to = target(me, slot)
            pltpu.make_async_remote_copy(
                src.at[to, :, pl.ds(begin, width)],
                dst.at[slot, :, pl.ds(begin, width)],
                sem_s,
                sem_r.at[lax.div(slot, GROUP)],
                device_id=(to,),
                device_id_type=MESH,
            ).start()
            return 0

        lax.fori_loop(1, DEV, body, 0)
        pltpu.make_async_copy(
            src.at[me, :, pl.ds(begin, width)], dst.at[0, :, pl.ds(begin, width)], sem_r.at[0]
        ).start()

    (a0, a1), (_, a2) = PARTS_A
    loads[0].wait()
    turn_blocks(16, 0, 3, send_a)
    pl.semaphore_wait(barrier, DEV - 1)
    send_part(send_a, recv_a, a0, a1 - a0, send_sem.at[0], recv_sem_a.at[0])
    loads[1].wait()
    loads[2].wait()
    turn_blocks(16, 3, 9, send_a)
    for r in range(PAIRS):
        gap = jnp.zeros((HALF - TAIL, 128), BF16)
        both = [xin[16 + r, MAIN:NG, :], gap, xin[r, MAIN:NG, :], gap]
        turn[1, :, r, :] = turned(jnp.concatenate(both, axis=0))
    send_a[:, :, MAIN:LANES_A] = turn[1].astype(BF16)
    send_part(send_a, recv_a, a1, a2 - a1, send_sem.at[1], recv_sem_a.at[1])
    loads[3].wait()
    turn_blocks(0, 0, 9, send_b)
    send_part(send_b, recv_b, 0, LANES_B, send_sem.at[2], recv_sem_b)

    loads[4].wait()
    w_wide[...] = jnp.zeros_like(w_wide)
    w_wide[pl.ds(HALF, TAIL), pl.ds(0, NG)] = w_in[pl.ds(MAIN, TAIL), :]
    w_wide[pl.ds(128, MAIN), pl.ds(0, NG)] = w_in[pl.ds(0, MAIN), :]
    spread[...] = same_block((256, 256), 1, 16, 1, 16).astype(BF16)

    def screen(g, _):
        slots = pl.ds(g * GROUP, GROUP)
        for p, (begin, end) in enumerate(PARTS_A):
            view = recv_a.at[slots, :, pl.ds(begin, end - begin)]
            pltpu.make_async_copy(view, view, recv_sem_a.at[p, g]).wait()
        left = recv_a[slots].reshape(GROUP * PAIRS, LANES_A)

        def column(n, _):
            rows = pl.ds(pl.multiple_of(n * 256, 256), 256)
            part = lax.dot_general(left, w_wide[rows, :], (((1,), (1,)), ((), ())), preferred_element_type=F32)
            screened[g, :, rows] = part.astype(BF16)
            return 0

        lax.fori_loop(0, 5, column, 0)
        return 0

    lax.fori_loop(0, GROUPS, screen, 0)

    def contract(g, _):
        slots = pl.ds(g * GROUP, GROUP)
        view = recv_b.at[slots]
        pltpu.make_async_copy(view, view, recv_sem_b.at[g]).wait()
        tails = recv_a[slots, :, MAIN:LANES_A].reshape(GROUP * PAIRS, 128)
        mains = recv_b[slots].reshape(GROUP * PAIRS, MAIN)
        nt = (((1,), (1,)), ((), ()))
        every = lax.dot_general(mains, screened[g, :, 128:], nt, preferred_element_type=F32)
        every = every + lax.dot_general(tails, screened[g, :, :128], nt, preferred_element_type=F32)
        own = jnp.where(same_block((256, 256), 16, 0, 16, 0), every, 0.0).astype(BF16)
        wide = jnp.dot(own, spread[...], preferred_element_type=F32)
        wide = jnp.where(same_block((256, 256), 1, 16, 16, 0), wide, 0.0).astype(BF16)
        gather = same_block((GROUP, 256), 1, GROUP, 16, 0).astype(BF16)
        rows = jnp.dot(gather, wide, preferred_element_type=F32)
        staged[slots, 0, :] = rows[:, :128]
        staged[slots, 1, :] = rows[:, 128:]

        def give_back(i, _):
            slot = g * GROUP + i
            to = origin(me, slot)
            pltpu.make_async_remote_copy(
                staged.at[slot], landed.at[me], back_send_sem, back_recv_sem,
                device_id=(to,), device_id_type=MESH,
            ).start()
            return 0

        lax.fori_loop(jnp.where(g == 0, 1, 0), GROUP, give_back, 0)
        return 0

    lax.fori_loop(0, GROUPS, contract, 0)
    pltpu.make_async_copy(staged.at[0], landed.at[me], back_recv_sem).start()

    for p, (begin, end) in enumerate(PARTS_A):
        view = send_a.at[pl.ds(1, DEV - 1), :, pl.ds(begin, end - begin)]
        pltpu.make_async_copy(view, view, send_sem.at[p]).wait()
    view = send_b.at[pl.ds(1, DEV - 1)]
    pltpu.make_async_copy(view, view, send_sem.at[2]).wait()
    view = staged.at[pl.ds(1, DEV - 1)]
    pltpu.make_async_copy(view, view, back_send_sem).wait()
    pltpu.make_async_copy(landed, landed, back_recv_sem).wait()
    o_ref[:, :128] = landed[:, 0, :]
    o_ref[:, 128:] = landed[:, 1, :]


def on_device(densities, screening, live):
    x = jnp.transpose(densities, (1, 2, 3, 0))[0]
    blocks = pl.pallas_call(
        kernel,
        out_shape=jax.ShapeDtypeStruct((DEV, PAIRS * PAIRS), F32),
        in_specs=[pl.BlockSpec(memory_space=pl.ANY)] * 2,
        out_specs=pl.BlockSpec(memory_space=pltpu.VMEM),
        scratch_shapes=[
            pltpu.VMEM((2 * PAIRS, NG, DEV), BF16),
            pltpu.VMEM((NG, NG), BF16),
            pltpu.VMEM((LANES_A, LANES_A), BF16),
            pltpu.VMEM((DEV, PAIRS, LANES_A), BF16),
            pltpu.VMEM((DEV, PAIRS, LANES_B), BF16),
            pltpu.VMEM((DEV, PAIRS, LANES_A), BF16),
            pltpu.VMEM((DEV, PAIRS, LANES_B), BF16),
            pltpu.VMEM((GROUPS, GROUP * PAIRS, LANES_A), BF16),
            pltpu.VMEM((2, DEV, PAIRS, 128), F32),
            pltpu.VMEM((256, 256), BF16),
            pltpu.VMEM((DEV, 2, 128), F32),
            pltpu.VMEM((DEV, 2, 128), F32),
            pltpu.SemaphoreType.DMA((5,)),
            pltpu.SemaphoreType.DMA((3,)),
            pltpu.SemaphoreType.DMA((2, GROUPS)),
            pltpu.SemaphoreType.DMA((GROUPS,)),
            pltpu.SemaphoreType.DMA,
            pltpu.SemaphoreType.DMA,
        ],
        compiler_params=pltpu.CompilerParams(
            collective_id=0, has_side_effects=True, vmem_limit_bytes=58 << 20
        ),
    )(x, screening[0])
    return (blocks * live.astype(F32)).astype(BF16)[:, None, :]


def solution(mesh):
    in_specs = (P(None, "pb", None, None), P("pb", None, None), P(None, "pb"))
    return jax.shard_map(
        on_device, mesh=mesh, in_specs=in_specs, out_specs=P(None, "pb", None), check_vma=False
    )
```

```python
import jax
import jax.numpy as jnp
from jax import lax
from jax.experimental import pallas as pl
from jax.experimental.pallas import tpu as pltpu
from jax.sharding import PartitionSpec as P

F32 = jnp.float32
BF16 = jnp.bfloat16
MESH = pl.DeviceIdType.MESH

DEV = 128
PAIRS = 16
NG = 1200
MAIN = 1152
TAIL = NG - MAIN
HALF = 64
LANES_A = MAIN + 128
LANES_B = MAIN
STEP = 37
GROUP = 16
GROUPS = DEV // GROUP
FEW = 8
FEWS = DEV // FEW
ROWS = FEW * PAIRS
PARTS_A = ((0, 384), (384, LANES_A))


def digits(i):
    return i // 32, i // 8 % 4, i // 2 % 4, i % 2


def hops(i):
    return sum(min(d, 4 - d) for d in digits(i)[:3])


_MIXED = [i * STEP % DEV for i in range(1, DEV)]
ORDER = [0] + sorted(_MIXED, key=lambda i: hops(i) <= 1)


def fill_places(me, to_ref, from_ref):
    z, x, y, c = lax.div(me, 32), lax.rem(lax.div(me, 8), 4), lax.rem(lax.div(me, 2), 4), lax.rem(me, 2)
    at = [
        [lax.rem(own + d, size) * unit for d in range(size)]
        for own, size, unit in ((z, 4, 32), (x, 4, 8), (y, 4, 2), (c, 2, 1))
    ]
    for slot, offset in enumerate(ORDER):
        there = digits(offset)
        back = [-d % size for d, size in zip(there, (4, 4, 4, 2))]
        to_ref[slot] = sum(column[d] for column, d in zip(at, there))
        from_ref[slot] = sum(column[d] for column, d in zip(at, back))


def same_block(shape, div0, mod0, div1, mod1):
    row = lax.broadcasted_iota(jnp.int32, shape, 0)
    col = lax.broadcasted_iota(jnp.int32, shape, 1)
    row = row // div0 if div0 > 1 else row % mod0
    col = col // div1 if div1 > 1 else col % mod1
    return row == col


def kernel(
    x_hbm, w_hbm, live_ref, o_ref,
    xin, w_in, w_wide, send_a, send_b, recv_a, recv_b, screened, turn, spread, staged, landed,
    to_ref, from_ref, load_sem, send_sem, recv_sem_a, recv_sem_b, back_send_sem, back_recv_sem,
):
    me = lax.axis_index("pb")

    loads = [
        pltpu.make_async_copy(x_hbm.at[pl.ds(16, 16), pl.ds(0, 384)], xin.at[pl.ds(16, 16), pl.ds(0, 384)], load_sem.at[0]),
        pltpu.make_async_copy(x_hbm.at[pl.ds(16, 16), pl.ds(384, 816)], xin.at[pl.ds(16, 16), pl.ds(384, 816)], load_sem.at[1]),
        pltpu.make_async_copy(x_hbm.at[pl.ds(0, 16), pl.ds(MAIN, TAIL)], xin.at[pl.ds(0, 16), pl.ds(MAIN, TAIL)], load_sem.at[2]),
        pltpu.make_async_copy(x_hbm.at[pl.ds(0, 16), pl.ds(0, MAIN)], xin.at[pl.ds(0, 16), pl.ds(0, MAIN)], load_sem.at[3]),
        pltpu.make_async_copy(w_hbm, w_in, load_sem.at[4]),
    ]
    for load in loads:
        load.start()

    barrier = pltpu.get_barrier_semaphore()

    def greet(slot, _):
        pl.semaphore_signal(barrier, inc=1, device_id=(lax.rem(me + slot, DEV),), device_id_type=MESH)
        return 0

    lax.fori_loop(1, DEV, greet, 0)

    fill_places(me, to_ref, from_ref)

    def turned(block):
        return jnp.transpose(block).astype(F32)

    def turn_block(first_row, column, slot, out, out_column):
        for r in range(PAIRS):
            turn[slot, :, r, :] = turned(xin[first_row + r, pl.ds(column, 128), :])
        out[:, :, pl.ds(out_column, 128)] = turn[slot].astype(BF16)

    def turn_blocks(first_row, begin, end, out):
        def body(j, _):
            column = pl.multiple_of(j * 128, 128)
            turn_block(first_row, column, lax.rem(j, 2), out, column)
            return 0

        lax.fori_loop(begin, end, body, 0)

    def send_part(src, dst, begin, width, sem_s, sem_r, group):
        def body(slot, _):
            to = to_ref[slot]
            pltpu.make_async_remote_copy(
                src.at[to, :, pl.ds(begin, width)],
                dst.at[slot, :, pl.ds(begin, width)],
                sem_s,
                sem_r.at[lax.div(slot, group)],
                device_id=(to,),
                device_id_type=MESH,
            ).start()
            return 0

        lax.fori_loop(1, DEV, body, 0)
        pltpu.make_async_copy(
            src.at[me, :, pl.ds(begin, width)], dst.at[0, :, pl.ds(begin, width)], sem_r.at[0]
        ).start()

    (a0, a1), (_, a2) = PARTS_A
    loads[0].wait()
    turn_blocks(16, 0, 3, send_a)
    pl.semaphore_wait(barrier, DEV - 1)
    send_part(send_a, recv_a, a0, a1 - a0, send_sem.at[0], recv_sem_a.at[0], GROUP)
    loads[1].wait()
    loads[2].wait()
    turn_blocks(16, 3, 9, send_a)
    for r in range(PAIRS):
        gap = jnp.zeros((HALF - TAIL, 128), BF16)
        both = [xin[16 + r, MAIN:NG, :], gap, xin[r, MAIN:NG, :], gap]
        turn[1, :, r, :] = turned(jnp.concatenate(both, axis=0))
    send_a[:, :, MAIN:LANES_A] = turn[1].astype(BF16)
    send_part(send_a, recv_a, a1, a2 - a1, send_sem.at[1], recv_sem_a.at[1], GROUP)
    loads[3].wait()
    turn_blocks(0, 0, 9, send_b)
    send_part(send_b, recv_b, 0, LANES_B, send_sem.at[2], recv_sem_b, FEW)

    loads[4].wait()
    w_wide[...] = jnp.zeros_like(w_wide)
    w_wide[pl.ds(HALF, TAIL), pl.ds(0, NG)] = w_in[pl.ds(MAIN, TAIL), :]
    w_wide[pl.ds(128, MAIN), pl.ds(0, NG)] = w_in[pl.ds(0, MAIN), :]
    spread[...] = same_block((ROWS, 256), 1, 16, 1, 16).astype(BF16)

    def screen(g, _):
        slots = pl.ds(g * GROUP, GROUP)
        for p, (begin, end) in enumerate(PARTS_A):
            view = recv_a.at[slots, :, pl.ds(begin, end - begin)]
            pltpu.make_async_copy(view, view, recv_sem_a.at[p, g]).wait()
        left = recv_a[slots].reshape(GROUP * PAIRS, LANES_A)

        def column(n, _):
            rows = pl.ds(pl.multiple_of(n * 256, 256), 256)
            part = lax.dot_general(left, w_wide[rows, :], (((1,), (1,)), ((), ())), preferred_element_type=F32)
            screened[pl.ds(g * GROUP * PAIRS, GROUP * PAIRS), rows] = part.astype(BF16)
            return 0

        lax.fori_loop(0, 5, column, 0)
        return 0

    lax.fori_loop(0, GROUPS, screen, 0)

    def contract(g, _):
        slots = pl.ds(g * FEW, FEW)
        view = recv_b.at[slots]
        pltpu.make_async_copy(view, view, recv_sem_b.at[g]).wait()
        tails = recv_a[slots, :, MAIN:LANES_A].reshape(ROWS, 128)
        mains = recv_b[slots].reshape(ROWS, MAIN)
        right = screened[pl.ds(g * ROWS, ROWS), :]
        nt = (((1,), (1,)), ((), ()))
        every = lax.dot_general(mains, right[:, 128:], nt, preferred_element_type=F32)
        every = every + lax.dot_general(tails, right[:, :128], nt, preferred_element_type=F32)
        own = jnp.where(same_block((ROWS, ROWS), 16, 0, 16, 0), every, 0.0).astype(BF16)
        wide = jnp.dot(own, spread[...], preferred_element_type=F32)
        wide = jnp.where(same_block((ROWS, 256), 1, 16, 16, 0), wide, 0.0).astype(BF16)
        gather = same_block((FEW, ROWS), 1, FEW, 16, 0).astype(BF16)
        rows = jnp.dot(gather, wide, preferred_element_type=F32)
        staged[slots, 0, :] = rows[:, :128]
        staged[slots, 1, :] = rows[:, 128:]

        def give_back(i, _):
            slot = g * FEW + i
            pltpu.make_async_remote_copy(
                staged.at[slot], landed.at[me], back_send_sem, back_recv_sem,
                device_id=(from_ref[slot],), device_id_type=MESH,
            ).start()
            return 0

        lax.fori_loop(jnp.where(g == 0, 1, 0), FEW, give_back, 0)
        return 0

    kept = jnp.where(same_block((DEV, DEV), 1, DEV, 1, DEV), live_ref[...].astype(F32), 0.0).astype(BF16)

    def keep(rows):
        return jnp.dot(kept, rows.astype(BF16), preferred_element_type=F32).astype(BF16)

    lax.fori_loop(0, FEWS, contract, 0)
    pltpu.make_async_copy(staged.at[0], landed.at[me], back_recv_sem).start()

    for p, (begin, end) in enumerate(PARTS_A):
        view = send_a.at[pl.ds(1, DEV - 1), :, pl.ds(begin, end - begin)]
        pltpu.make_async_copy(view, view, send_sem.at[p]).wait()
    view = send_b.at[pl.ds(1, DEV - 1)]
    pltpu.make_async_copy(view, view, send_sem.at[2]).wait()
    view = staged.at[pl.ds(1, DEV - 1)]
    pltpu.make_async_copy(view, view, back_send_sem).wait()
    pltpu.make_async_copy(landed, landed, back_recv_sem).wait()
    o_ref[:, :128] = keep(landed[:, 0, :])
    o_ref[:, 128:] = keep(landed[:, 1, :])


def on_device(densities, screening, live):
    x = jnp.transpose(densities, (1, 2, 3, 0))[0]
    blocks = pl.pallas_call(
        kernel,
        out_shape=jax.ShapeDtypeStruct((DEV, PAIRS * PAIRS), BF16),
        in_specs=[pl.BlockSpec(memory_space=pl.ANY)] * 2 + [pl.BlockSpec(memory_space=pltpu.VMEM)],
        out_specs=pl.BlockSpec(memory_space=pltpu.VMEM),
        scratch_shapes=[
            pltpu.VMEM((2 * PAIRS, NG, DEV), BF16),
            pltpu.VMEM((NG, NG), BF16),
            pltpu.VMEM((LANES_A, LANES_A), BF16),
            pltpu.VMEM((DEV, PAIRS, LANES_A), BF16),
            pltpu.VMEM((DEV, PAIRS, LANES_B), BF16),
            pltpu.VMEM((DEV, PAIRS, LANES_A), BF16),
            pltpu.VMEM((DEV, PAIRS, LANES_B), BF16),
            pltpu.VMEM((DEV * PAIRS, LANES_A), BF16),
            pltpu.VMEM((2, DEV, PAIRS, 128), F32),
            pltpu.VMEM((ROWS, 256), BF16),
            pltpu.VMEM((DEV, 2, 128), F32),
            pltpu.VMEM((DEV, 2, 128), F32),
            pltpu.SMEM((DEV,), jnp.int32),
            pltpu.SMEM((DEV,), jnp.int32),
            pltpu.SemaphoreType.DMA((5,)),
            pltpu.SemaphoreType.DMA((3,)),
            pltpu.SemaphoreType.DMA((2, GROUPS)),
            pltpu.SemaphoreType.DMA((FEWS,)),
            pltpu.SemaphoreType.DMA,
            pltpu.SemaphoreType.DMA,
        ],
        compiler_params=pltpu.CompilerParams(
            collective_id=0, has_side_effects=True, vmem_limit_bytes=58 << 20
        ),
    )(x, screening[0], live.reshape(1, DEV))
    return blocks[:, None, :]


def solution(mesh):
    in_specs = (P(None, "pb", None, None), P("pb", None, None), P(None, "pb"))
    return jax.shard_map(
        on_device, mesh=mesh, in_specs=in_specs, out_specs=P(None, "pb", None), check_vma=False
    )
```

```python
import jax
import jax.numpy as jnp
from jax import lax
from jax.experimental import pallas as pl
from jax.experimental.pallas import tpu as pltpu
from jax.sharding import PartitionSpec as P

F32 = jnp.float32
BF16 = jnp.bfloat16
MESH = pl.DeviceIdType.MESH

DEV = 128
PAIRS = 16
NG = 1200
MAIN = 1152
TAIL = NG - MAIN
HALF = 64
LANES_A = MAIN + 128
LANES_B = MAIN
STEP = 37
GROUP = 16
GROUPS = DEV // GROUP
FEW = 8
FEWS = DEV // FEW
ROWS = FEW * PAIRS
PARTS_A = ((0, 384), (384, LANES_A))


def digits(i):
    return i // 32, i // 8 % 4, i // 2 % 4, i % 2


def hops(i):
    return sum(min(d, 4 - d) for d in digits(i)[:3])


_MIXED = [i * STEP % DEV for i in range(1, DEV)]
ORDER = [0] + sorted(_MIXED, key=lambda i: hops(i) <= 1)


def fill_places(me, to_ref, from_ref):
    z, x, y, c = lax.div(me, 32), lax.rem(lax.div(me, 8), 4), lax.rem(lax.div(me, 2), 4), lax.rem(me, 2)
    at = [
        [lax.rem(own + d, size) * unit for d in range(size)]
        for own, size, unit in ((z, 4, 32), (x, 4, 8), (y, 4, 2), (c, 2, 1))
    ]
    for slot, offset in enumerate(ORDER):
        there = digits(offset)
        back = [-d % size for d, size in zip(there, (4, 4, 4, 2))]
        to_ref[slot] = sum(column[d] for column, d in zip(at, there))
        from_ref[slot] = sum(column[d] for column, d in zip(at, back))


def same_block(shape, div0, mod0, div1, mod1):
    row = lax.broadcasted_iota(jnp.int32, shape, 0)
    col = lax.broadcasted_iota(jnp.int32, shape, 1)
    row = row // div0 if div0 > 1 else row % mod0
    col = col // div1 if div1 > 1 else col % mod1
    return row == col


def kernel(
    x_hbm, w_hbm, live_ref, o_ref,
    xin, w_in, w_wide, send_a, send_b, recv_a, recv_b, screened, turn, spread, kept, staged, landed,
    to_ref, from_ref, load_sem, send_sem, recv_sem_a, recv_sem_b, back_send_sem, back_recv_sem,
):
    me = lax.axis_index("pb")

    loads = [
        pltpu.make_async_copy(x_hbm.at[pl.ds(16, 16), pl.ds(0, 384)], xin.at[pl.ds(16, 16), pl.ds(0, 384)], load_sem.at[0]),
        pltpu.make_async_copy(x_hbm.at[pl.ds(16, 16), pl.ds(384, 816)], xin.at[pl.ds(16, 16), pl.ds(384, 816)], load_sem.at[1]),
        pltpu.make_async_copy(x_hbm.at[pl.ds(0, 16), pl.ds(MAIN, TAIL)], xin.at[pl.ds(0, 16), pl.ds(MAIN, TAIL)], load_sem.at[2]),
        pltpu.make_async_copy(x_hbm.at[pl.ds(0, 16), pl.ds(0, MAIN)], xin.at[pl.ds(0, 16), pl.ds(0, MAIN)], load_sem.at[3]),
        pltpu.make_async_copy(w_hbm, w_in, load_sem.at[4]),
    ]
    for load in loads:
        load.start()

    barrier = pltpu.get_barrier_semaphore()

    def greet(slot, _):
        pl.semaphore_signal(barrier, inc=1, device_id=(lax.rem(me + slot, DEV),), device_id_type=MESH)
        return 0

    lax.fori_loop(1, DEV, greet, 0)

    fill_places(me, to_ref, from_ref)

    def turned(block):
        return jnp.transpose(block).astype(F32)

    def turn_block(first_row, column, slot, out, out_column):
        for r in range(PAIRS):
            turn[slot, :, r, :] = turned(xin[first_row + r, pl.ds(column, 128), :])
        out[:, :, pl.ds(out_column, 128)] = turn[slot].astype(BF16)

    def turn_blocks(first_row, begin, end, out):
        def body(j, _):
            column = pl.multiple_of(j * 128, 128)
            turn_block(first_row, column, lax.rem(j, 2), out, column)
            return 0

        lax.fori_loop(begin, end, body, 0)

    def send_part(src, dst, begin, width, sem_s, sem_r, group):
        def body(slot, _):
            to = to_ref[slot]
            pltpu.make_async_remote_copy(
                src.at[to, :, pl.ds(begin, width)],
                dst.at[slot, :, pl.ds(begin, width)],
                sem_s,
                sem_r.at[lax.div(slot, group)],
                device_id=(to,),
                device_id_type=MESH,
            ).start()
            return 0

        lax.fori_loop(1, DEV, body, 0)
        pltpu.make_async_copy(
            src.at[me, :, pl.ds(begin, width)], dst.at[0, :, pl.ds(begin, width)], sem_r.at[0]
        ).start()

    (a0, a1), (_, a2) = PARTS_A
    loads[0].wait()
    turn_blocks(16, 0, 3, send_a)
    pl.semaphore_wait(barrier, DEV - 1)
    send_part(send_a, recv_a, a0, a1 - a0, send_sem.at[0], recv_sem_a.at[0], GROUP)
    loads[1].wait()
    loads[2].wait()
    turn_blocks(16, 3, 9, send_a)
    for r in range(PAIRS):
        gap = jnp.zeros((HALF - TAIL, 128), BF16)
        both = [xin[16 + r, MAIN:NG, :], gap, xin[r, MAIN:NG, :], gap]
        turn[1, :, r, :] = turned(jnp.concatenate(both, axis=0))
    send_a[:, :, MAIN:LANES_A] = turn[1].astype(BF16)
    send_part(send_a, recv_a, a1, a2 - a1, send_sem.at[1], recv_sem_a.at[1], GROUP)
    loads[3].wait()
    turn_blocks(0, 0, 9, send_b)
    send_part(send_b, recv_b, 0, LANES_B, send_sem.at[2], recv_sem_b, FEW)

    loads[4].wait()
    w_wide[...] = jnp.zeros_like(w_wide)
    w_wide[pl.ds(HALF, TAIL), pl.ds(0, NG)] = w_in[pl.ds(MAIN, TAIL), :]
    w_wide[pl.ds(128, MAIN), pl.ds(0, NG)] = w_in[pl.ds(0, MAIN), :]
    spread[...] = same_block((ROWS, 256), 1, 16, 1, 16).astype(BF16)

    def screen(g, _):
        slots = pl.ds(g * GROUP, GROUP)
        for p, (begin, end) in enumerate(PARTS_A):
            view = recv_a.at[slots, :, pl.ds(begin, end - begin)]
            pltpu.make_async_copy(view, view, recv_sem_a.at[p, g]).wait()
        left = recv_a[slots].reshape(GROUP * PAIRS, LANES_A)

        def column(n, _):
            rows = pl.ds(pl.multiple_of(n * 256, 256), 256)
            part = lax.dot_general(left, w_wide[rows, :], (((1,), (1,)), ((), ())), preferred_element_type=F32)
            screened[pl.ds(g * GROUP * PAIRS, GROUP * PAIRS), rows] = part.astype(BF16)
            return 0

        lax.fori_loop(0, 5, column, 0)
        return 0

    lax.fori_loop(0, GROUPS, screen, 0)

    def contract(g, _):
        slots = pl.ds(g * FEW, FEW)
        nt = (((1,), (1,)), ((), ()))
        tails = recv_a[slots, :, MAIN:LANES_A].reshape(ROWS, 128)
        right = screened[pl.ds(g * ROWS, ROWS), :]
        early = lax.dot_general(tails, right[:, :128], nt, preferred_element_type=F32)
        view = recv_b.at[slots]
        pltpu.make_async_copy(view, view, recv_sem_b.at[g]).wait()
        mains = recv_b[slots].reshape(ROWS, MAIN)
        every = early + lax.dot_general(mains, right[:, 128:], nt, preferred_element_type=F32)
        own = jnp.where(same_block((ROWS, ROWS), 16, 0, 16, 0), every, 0.0).astype(BF16)
        wide = jnp.dot(own, spread[...], preferred_element_type=F32)
        wide = jnp.where(same_block((ROWS, 256), 1, 16, 16, 0), wide, 0.0).astype(BF16)
        gather = same_block((FEW, ROWS), 1, FEW, 16, 0).astype(BF16)
        rows = jnp.dot(gather, wide, preferred_element_type=F32)
        staged[slots, 0, :] = rows[:, :128]
        staged[slots, 1, :] = rows[:, 128:]

        def give_back(i, _):
            slot = g * FEW + i
            pltpu.make_async_remote_copy(
                staged.at[slot], landed.at[me], back_send_sem, back_recv_sem,
                device_id=(from_ref[slot],), device_id_type=MESH,
            ).start()
            return 0

        @pl.when(g > 0)
        def _():
            give_back(0, 0)

        for i in range(1, FEW):
            give_back(i, 0)
        return 0

    ones = jnp.ones((DEV, 128), BF16)
    diagonal = jnp.where(same_block((DEV, DEV), 1, DEV, 1, DEV), live_ref[...].astype(F32), 0.0).astype(BF16)
    kept[...] = jnp.dot(diagonal, ones, preferred_element_type=F32)

    lax.fori_loop(0, FEWS, contract, 0)
    pltpu.make_async_copy(staged.at[0], landed.at[me], back_recv_sem).start()

    for p, (begin, end) in enumerate(PARTS_A):
        view = send_a.at[pl.ds(1, DEV - 1), :, pl.ds(begin, end - begin)]
        pltpu.make_async_copy(view, view, send_sem.at[p]).wait()
    view = send_b.at[pl.ds(1, DEV - 1)]
    pltpu.make_async_copy(view, view, send_sem.at[2]).wait()
    view = staged.at[pl.ds(1, DEV - 1)]
    pltpu.make_async_copy(view, view, back_send_sem).wait()
    pltpu.make_async_copy(landed, landed, back_recv_sem).wait()
    o_ref[:, :128] = (landed[:, 0, :] * kept[...]).astype(BF16)
    o_ref[:, 128:] = (landed[:, 1, :] * kept[...]).astype(BF16)


def on_device(densities, screening, live):
    x = jnp.transpose(densities, (1, 2, 3, 0))[0]
    blocks = pl.pallas_call(
        kernel,
        out_shape=jax.ShapeDtypeStruct((DEV, PAIRS * PAIRS), BF16),
        in_specs=[pl.BlockSpec(memory_space=pltpu.HBM)] * 2 + [pl.BlockSpec(memory_space=pltpu.VMEM)],
        out_specs=pl.BlockSpec(memory_space=pltpu.VMEM),
        scratch_shapes=[
            pltpu.VMEM((2 * PAIRS, NG, DEV), BF16),
            pltpu.VMEM((NG, NG), BF16),
            pltpu.VMEM((LANES_A, LANES_A), BF16),
            pltpu.VMEM((DEV, PAIRS, LANES_A), BF16),
            pltpu.VMEM((DEV, PAIRS, LANES_B), BF16),
            pltpu.VMEM((DEV, PAIRS, LANES_A), BF16),
            pltpu.VMEM((DEV, PAIRS, LANES_B), BF16),
            pltpu.VMEM((DEV * PAIRS, LANES_A), BF16),
            pltpu.VMEM((2, DEV, PAIRS, 128), F32),
            pltpu.VMEM((ROWS, 256), BF16),
            pltpu.VMEM((DEV, 128), F32),
            pltpu.VMEM((DEV, 2, 128), F32),
            pltpu.VMEM((DEV, 2, 128), F32),
            pltpu.SMEM((DEV,), jnp.int32),
            pltpu.SMEM((DEV,), jnp.int32),
            pltpu.SemaphoreType.DMA((5,)),
            pltpu.SemaphoreType.DMA((3,)),
            pltpu.SemaphoreType.DMA((2, GROUPS)),
            pltpu.SemaphoreType.DMA((FEWS,)),
            pltpu.SemaphoreType.DMA,
            pltpu.SemaphoreType.DMA,
        ],
        compiler_params=pltpu.CompilerParams(
            collective_id=0, has_side_effects=True, vmem_limit_bytes=52 << 20
        ),
    )(x, screening[0], live.reshape(1, DEV))
    return blocks[:, None, :]


def solution(mesh):
    in_specs = (P(None, "pb", None, None), P("pb", None, None), P(None, "pb"))
    return jax.shard_map(
        on_device, mesh=mesh, in_specs=in_specs, out_specs=P(None, "pb", None), check_vma=False
    )
```

```python
import jax
import jax.numpy as jnp
from jax import lax
from jax.experimental import pallas as pl
from jax.experimental.pallas import tpu as pltpu
from jax.sharding import PartitionSpec as P

F32 = jnp.float32
BF16 = jnp.bfloat16
MESH = pl.DeviceIdType.MESH

DEV = 128
PAIRS = 16
NG = 1200
MAIN = 1152
TAIL = NG - MAIN
LANES_A = MAIN + 128
FULL = 12
THIRD = 128 - 2 * TAIL
LANES_B = MAIN
STEP = 37
GROUP = 16
GROUPS = DEV // GROUP
FEW = 8
FEWS = DEV // FEW
ROWS = FEW * PAIRS
FIRST = 384
REST = MAIN - FIRST


def digits(i):
    return i // 32, i // 8 % 4, i // 2 % 4, i % 2


def hops(i):
    return sum(min(d, 4 - d) for d in digits(i)[:3])


_MIXED = [i * STEP % DEV for i in range(1, DEV)]
ORDER = [0] + sorted(_MIXED, key=lambda i: hops(i) <= 1)


def fill_places(me, to_ref, from_ref):
    z, x, y, c = lax.div(me, 32), lax.rem(lax.div(me, 8), 4), lax.rem(lax.div(me, 2), 4), lax.rem(me, 2)
    at = [
        [lax.rem(own + d, size) * unit for d in range(size)]
        for own, size, unit in ((z, 4, 32), (x, 4, 8), (y, 4, 2), (c, 2, 1))
    ]
    for slot, offset in enumerate(ORDER):
        there = digits(offset)
        back = [-d % size for d, size in zip(there, (4, 4, 4, 2))]
        to_ref[slot] = sum(column[d] for column, d in zip(at, there))
        from_ref[slot] = sum(column[d] for column, d in zip(at, back))


def same_block(shape, div0, mod0, div1, mod1):
    row = lax.broadcasted_iota(jnp.int32, shape, 0)
    col = lax.broadcasted_iota(jnp.int32, shape, 1)
    row = row // div0 if div0 > 1 else row % mod0
    col = col // div1 if div1 > 1 else col % mod1
    return row == col


def kernel(
    x_hbm, w_hbm, live_hbm, o_ref,
    xin, w_in, w_wide, send_a, send_m, send_t, send_b, recv_a, recv_m, recv_t, recv_b, tails, lift, shift, screened, turn, spread, live_ref, kept, staged, landed,
    to_ref, from_ref, load_sem, send_sem, recv_sem_a, recv_sem_b, back_send_sem, back_recv_sem,
):
    me = lax.axis_index("pb")

    loads = [
        pltpu.make_async_copy(x_hbm.at[pl.ds(16, 16), pl.ds(0, FIRST)], xin.at[pl.ds(16, 16), pl.ds(0, FIRST)], load_sem.at[0]),
        pltpu.make_async_copy(x_hbm.at[pl.ds(16, 16), pl.ds(FIRST, NG - FIRST)], xin.at[pl.ds(16, 16), pl.ds(FIRST, NG - FIRST)], load_sem.at[1]),
        pltpu.make_async_copy(x_hbm.at[pl.ds(0, 16), pl.ds(MAIN, TAIL)], xin.at[pl.ds(0, 16), pl.ds(MAIN, TAIL)], load_sem.at[2]),
        pltpu.make_async_copy(x_hbm.at[pl.ds(0, 16), pl.ds(0, MAIN)], xin.at[pl.ds(0, 16), pl.ds(0, MAIN)], load_sem.at[3]),
        pltpu.make_async_copy(w_hbm, w_in, load_sem.at[4]),
        pltpu.make_async_copy(live_hbm, live_ref, load_sem.at[5]),
    ]
    for load in loads:
        load.start()

    recv_t[...] = jnp.zeros_like(recv_t)
    barrier = pltpu.get_barrier_semaphore()

    def greet(slot, _):
        pl.semaphore_signal(barrier, inc=1, device_id=(lax.rem(me + slot, DEV),), device_id_type=MESH)
        return 0

    for i in range(1, DEV):
        greet(i, 0)

    fill_places(me, to_ref, from_ref)

    def turned(block):
        return jnp.transpose(block).astype(F32)

    def turn_block(first_row, column, slot, out, out_column):
        for r in range(PAIRS):
            turn[slot, :, r, :] = turned(xin[first_row + r, pl.ds(column, 128), :])
        out[:, :, pl.ds(out_column, 128)] = turn[slot].astype(BF16)

    def turn_blocks(first_row, begin, end, out, left_out):
        def body(j, _):
            column = pl.multiple_of(j * 128, 128)
            turn_block(first_row, column, lax.rem(j, 2), out, pl.multiple_of(column - left_out, 128))
            return 0

        lax.fori_loop(begin, end, body, 0)

    def send_part(src, dst, sem_s, sem_r, group, rows=PAIRS):
        rows = pl.ds(0, rows)

        def body(slot, _):
            to = to_ref[slot]
            pltpu.make_async_remote_copy(
                src.at[to, rows], dst.at[slot, rows], sem_s, sem_r.at[lax.div(slot, group)],
                device_id=(to,), device_id_type=MESH,
            ).start()
            return 0

        lax.fori_loop(1, DEV, body, 0)
        pltpu.make_async_copy(src.at[me, rows], dst.at[0, rows], sem_r.at[0]).start()

    loads[0].wait()
    turn_blocks(16, 0, FIRST // 128, send_a, 0)
    pl.semaphore_wait(barrier, DEV - 1)
    send_part(send_a, recv_a, send_sem.at[0], recv_sem_a.at[0], GROUP)
    loads[1].wait()
    loads[2].wait()
    turn_blocks(16, FIRST // 128, 9, send_m, FIRST)
    send_part(send_m, recv_m, send_sem.at[1], recv_sem_a.at[1], GROUP)

    def tail_rows(r, begin, end):
        rows = [xin[PAIRS + r, MAIN + begin : MAIN + min(end, TAIL), :]] if begin < TAIL else []
        if end > TAIL:
            rows.append(xin[r, MAIN + max(begin - TAIL, 0) : MAIN + end - TAIL, :])
        return rows

    for r in range(FULL):
        begin = r % 3 * THIRD
        both = tail_rows(r, 0, 2 * TAIL) + tail_rows(FULL + r // 3, begin, begin + THIRD)
        turn[1, :, r, :] = turned(jnp.concatenate(both, axis=0))
    send_t[...] = turn[1].astype(BF16)
    send_part(send_t, recv_t, send_sem.at[3], recv_sem_a.at[2], GROUP, FULL)
    loads[3].wait()
    turn_blocks(0, 0, 9, send_b, 0)
    send_part(send_b, recv_b, send_sem.at[2], recv_sem_b, FEW)

    loads[4].wait()
    w_wide[...] = jnp.zeros_like(w_wide)
    w_wide[pl.ds(TAIL, TAIL), pl.ds(0, NG)] = w_in[pl.ds(MAIN, TAIL), :]
    w_wide[pl.ds(128, MAIN), pl.ds(0, NG)] = w_in[pl.ds(0, MAIN), :]
    spread[...] = same_block((ROWS, 256), 1, 16, 1, 16).astype(BF16)

    row = lax.broadcasted_iota(jnp.int32, (256, 256), 0)
    col = lax.broadcasted_iota(jnp.int32, (256, 256), 1)
    lane = lax.broadcasted_iota(jnp.int32, (128, 128), 0)
    goal = lax.broadcasted_iota(jnp.int32, (128, 128), 1)
    for c in range(3):
        same = (row // PAIRS == col // PAIRS) & (row % PAIRS >= FULL) & ((row % PAIRS - FULL) * 3 + c == col % PAIRS)
        lift[c] = same.astype(F32).astype(BF16)
        moved = (lane >= 2 * TAIL) & (lane - 2 * TAIL + c * THIRD == goal)
        shift[c] = moved.astype(F32).astype(BF16)

    def whole_tails(travelled):
        own = lax.broadcasted_iota(jnp.int32, (256, 128), 1) < 2 * TAIL
        total = jnp.where(own, travelled.astype(F32), 0.0)
        for c in range(3):
            third = jnp.dot(lift[c], travelled, preferred_element_type=F32).astype(BF16)
            total = total + jnp.dot(third, shift[c], preferred_element_type=F32)
        return total.astype(BF16)

    def screen(g, _):
        slots = pl.ds(g * GROUP, GROUP)
        for p, (part, rows) in enumerate(((recv_a, PAIRS), (recv_m, PAIRS), (recv_t, FULL))):
            view = part.at[slots, pl.ds(0, rows)]
            pltpu.make_async_copy(view, view, recv_sem_a.at[p, g]).wait()
        tail = whole_tails(recv_t[slots].reshape(GROUP * PAIRS, 128))
        tails[pl.ds(g * GROUP * PAIRS, GROUP * PAIRS), :] = tail
        main = jnp.concatenate([recv_a[slots], recv_m[slots]], axis=2).reshape(GROUP * PAIRS, MAIN)
        left = jnp.concatenate([main, tail], axis=1)

        def column(n, _):
            rows = pl.ds(pl.multiple_of(n * 256, 256), 256)
            part = lax.dot_general(left, w_wide[rows, :], (((1,), (1,)), ((), ())), preferred_element_type=F32)
            screened[pl.ds(g * GROUP * PAIRS, GROUP * PAIRS), rows] = part.astype(BF16)
            return 0

        lax.fori_loop(0, 5, column, 0)
        return 0

    lax.fori_loop(0, GROUPS, screen, 0)

    def contract(g, _):
        slots = pl.ds(g * FEW, FEW)
        nt = (((1,), (1,)), ((), ()))
        right = screened[pl.ds(g * ROWS, ROWS), :]
        early = lax.dot_general(tails[pl.ds(g * ROWS, ROWS), :], right[:, :128], nt, preferred_element_type=F32)
        view = recv_b.at[slots]
        pltpu.make_async_copy(view, view, recv_sem_b.at[g]).wait()
        mains = recv_b[slots].reshape(ROWS, MAIN)
        every = early + lax.dot_general(mains, right[:, 128:], nt, preferred_element_type=F32)
        own = jnp.where(same_block((ROWS, ROWS), 16, 0, 16, 0), every, 0.0).astype(BF16)
        wide = jnp.dot(own, spread[...], preferred_element_type=F32)
        wide = jnp.where(same_block((ROWS, 256), 1, 16, 16, 0), wide, 0.0).astype(BF16)
        gather = same_block((FEW, ROWS), 1, FEW, 16, 0).astype(BF16)
        rows = jnp.dot(gather, wide, preferred_element_type=F32)
        staged[slots, 0, :] = rows[:, :128]
        staged[slots, 1, :] = rows[:, 128:]

        def give_back(i, _):
            slot = g * FEW + i
            pltpu.make_async_remote_copy(
                staged.at[slot], landed.at[me], back_send_sem, back_recv_sem,
                device_id=(from_ref[slot],), device_id_type=MESH,
            ).start()
            return 0

        @pl.when(g > 0)
        def _():
            give_back(0, 0)

        for i in range(1, FEW):
            give_back(i, 0)
        return 0

    loads[5].wait()
    ones = jnp.ones((DEV, 128), BF16)
    diagonal = jnp.where(same_block((DEV, DEV), 1, DEV, 1, DEV), live_ref[...].astype(F32), 0.0).astype(BF16)
    kept[...] = jnp.dot(diagonal, ones, preferred_element_type=F32)

    lax.fori_loop(0, FEWS, contract, 0)
    pltpu.make_async_copy(staged.at[0], landed.at[me], back_recv_sem).start()

    for p, (part, rows) in enumerate(((send_a, PAIRS), (send_m, PAIRS), (send_b, PAIRS), (send_t, FULL))):
        view = part.at[pl.ds(1, DEV - 1), pl.ds(0, rows)]
        pltpu.make_async_copy(view, view, send_sem.at[p]).wait()
    view = staged.at[pl.ds(1, DEV - 1)]
    pltpu.make_async_copy(view, view, back_send_sem).wait()
    pltpu.make_async_copy(landed, landed, back_recv_sem).wait()
    o_ref[:, :128] = (landed[:, 0, :] * kept[...]).astype(BF16)
    o_ref[:, 128:] = (landed[:, 1, :] * kept[...]).astype(BF16)


def on_device(densities, screening, live):
    x = jnp.transpose(densities, (1, 2, 3, 0))[0]
    blocks = pl.pallas_call(
        kernel,
        out_shape=jax.ShapeDtypeStruct((DEV, PAIRS * PAIRS), BF16),
        in_specs=[pl.BlockSpec(memory_space=pltpu.HBM)] * 3,
        out_specs=pl.BlockSpec(memory_space=pltpu.VMEM),
        scratch_shapes=[
            pltpu.VMEM((2 * PAIRS, NG, DEV), BF16),
            pltpu.VMEM((NG, NG), BF16),
            pltpu.VMEM((LANES_A, LANES_A), BF16),
            pltpu.VMEM((DEV, PAIRS, FIRST), BF16),
            pltpu.VMEM((DEV, PAIRS, REST), BF16),
            pltpu.VMEM((DEV, PAIRS, 128), BF16),
            pltpu.VMEM((DEV, PAIRS, LANES_B), BF16),
            pltpu.VMEM((DEV, PAIRS, FIRST), BF16),
            pltpu.VMEM((DEV, PAIRS, REST), BF16),
            pltpu.VMEM((DEV, PAIRS, 128), BF16),
            pltpu.VMEM((DEV, PAIRS, LANES_B), BF16),
            pltpu.VMEM((DEV * PAIRS, 128), BF16),
            pltpu.VMEM((3, 256, 256), BF16),
            pltpu.VMEM((3, 128, 128), BF16),
            pltpu.VMEM((DEV * PAIRS, LANES_A), BF16),
            pltpu.VMEM((2, DEV, PAIRS, 128), F32),
            pltpu.VMEM((ROWS, 256), BF16),
            pltpu.VMEM((1, DEV), jnp.int32),
            pltpu.VMEM((DEV, 128), F32),
            pltpu.VMEM((DEV, 2, 128), F32),
            pltpu.VMEM((DEV, 2, 128), F32),
            pltpu.SMEM((DEV,), jnp.int32),
            pltpu.SMEM((DEV,), jnp.int32),
            pltpu.SemaphoreType.DMA((6,)),
            pltpu.SemaphoreType.DMA((4,)),
            pltpu.SemaphoreType.DMA((3, GROUPS)),
            pltpu.SemaphoreType.DMA((FEWS,)),
            pltpu.SemaphoreType.DMA,
            pltpu.SemaphoreType.DMA,
        ],
        compiler_params=pltpu.CompilerParams(
            collective_id=0, has_side_effects=True, vmem_limit_bytes=52 << 20
        ),
    )(x, screening[0], pltpu.with_memory_space_constraint(live.reshape(1, DEV), pltpu.HBM))
    return blocks[:, None, :]


def solution(mesh):
    in_specs = (P(None, "pb", None, None), P("pb", None, None), P(None, "pb"))
    return jax.shard_map(
        on_device, mesh=mesh, in_specs=in_specs, out_specs=P(None, "pb", None), check_vma=False
    )
```

```python
import jax
import jax.numpy as jnp
from jax import lax
from jax.experimental import pallas as pl
from jax.experimental.pallas import tpu as pltpu
from jax.sharding import PartitionSpec as P

F32 = jnp.float32
BF16 = jnp.bfloat16
MESH = pl.DeviceIdType.MESH

DEV = 128
PAIRS = 16
NG = 1200
MAIN = 1152
TAIL = NG - MAIN
LANES_A = MAIN + 128
HALF = PAIRS // 2
LANES_B = MAIN
STEP = 37
GROUP = 16
GROUPS = DEV // GROUP
FEW = 8
FEWS = DEV // FEW
ROWS = FEW * PAIRS
FIRST = 384
REST = MAIN - FIRST


def digits(i):
    return i // 32, i // 8 % 4, i // 2 % 4, i % 2


def hops(i):
    return sum(min(d, 4 - d) for d in digits(i)[:3])


_MIXED = [i * STEP % DEV for i in range(1, DEV)]
ORDER = [0] + sorted(_MIXED, key=lambda i: hops(i) <= 1)


def fill_places(me, to_ref, from_ref):
    z, x, y, c = lax.div(me, 32), lax.rem(lax.div(me, 8), 4), lax.rem(lax.div(me, 2), 4), lax.rem(me, 2)
    at = [
        [lax.rem(own + d, size) * unit for d in range(size)]
        for own, size, unit in ((z, 4, 32), (x, 4, 8), (y, 4, 2), (c, 2, 1))
    ]
    for slot, offset in enumerate(ORDER):
        there = digits(offset)
        back = [-d % size for d, size in zip(there, (4, 4, 4, 2))]
        to_ref[slot] = sum(column[d] for column, d in zip(at, there))
        from_ref[slot] = sum(column[d] for column, d in zip(at, back))


def same_block(shape, div0, mod0, div1, mod1):
    row = lax.broadcasted_iota(jnp.int32, shape, 0)
    col = lax.broadcasted_iota(jnp.int32, shape, 1)
    row = row // div0 if div0 > 1 else row % mod0
    col = col // div1 if div1 > 1 else col % mod1
    return row == col


def kernel(
    x_hbm, w_hbm, live_hbm, o_ref,
    xin, w_in, w_wide, send_a, send_m, send_t, recv_a, recv_m, recv_t, own_main, own_tail,
    screened, screened_t, recv_s, recv_st, turn, spread, live_ref, kept, landed,
    to_ref, from_ref, load_sem, send_sem, recv_sem_a, recv_sem_s,
):
    me = lax.axis_index("pb")

    loads = [
        pltpu.make_async_copy(x_hbm.at[pl.ds(16, 16), pl.ds(0, FIRST)], xin.at[pl.ds(16, 16), pl.ds(0, FIRST)], load_sem.at[0]),
        pltpu.make_async_copy(x_hbm.at[pl.ds(16, 16), pl.ds(FIRST, NG - FIRST)], xin.at[pl.ds(16, 16), pl.ds(FIRST, NG - FIRST)], load_sem.at[1]),
        pltpu.make_async_copy(x_hbm.at[pl.ds(0, 16), pl.ds(MAIN, TAIL)], xin.at[pl.ds(0, 16), pl.ds(MAIN, TAIL)], load_sem.at[2]),
        pltpu.make_async_copy(x_hbm.at[pl.ds(0, 16), pl.ds(0, MAIN)], xin.at[pl.ds(0, 16), pl.ds(0, MAIN)], load_sem.at[3]),
        pltpu.make_async_copy(w_hbm, w_in, load_sem.at[4]),
        pltpu.make_async_copy(live_hbm, live_ref, load_sem.at[5]),
    ]
    for load in loads:
        load.start()

    barrier = pltpu.get_barrier_semaphore()

    def greet(slot, _):
        pl.semaphore_signal(barrier, inc=1, device_id=(lax.rem(me + slot, DEV),), device_id_type=MESH)
        return 0

    for i in range(1, DEV):
        greet(i, 0)

    fill_places(me, to_ref, from_ref)

    def turned(block):
        return jnp.transpose(block).astype(F32)

    def turn_block(first_row, column, slot, out, out_column):
        for r in range(PAIRS):
            turn[slot, :, r, :] = turned(xin[first_row + r, pl.ds(column, 128), :])
        out[:, :, pl.ds(out_column, 128)] = turn[slot].astype(BF16)

    def turn_blocks(first_row, begin, end, out, left_out):
        def body(j, _):
            column = pl.multiple_of(j * 128, 128)
            turn_block(first_row, column, lax.rem(j, 2), out, pl.multiple_of(column - left_out, 128))
            return 0

        lax.fori_loop(begin, end, body, 0)

    def send_part(src, dst, sem_s, sem_r, group):

        def body(slot, _):
            to = to_ref[slot]
            pltpu.make_async_remote_copy(
                src.at[to], dst.at[slot], sem_s, sem_r.at[lax.div(slot, group)],
                device_id=(to,), device_id_type=MESH,
            ).start()
            return 0

        lax.fori_loop(1, DEV, body, 0)
        pltpu.make_async_copy(src.at[me], dst.at[0], sem_r.at[0]).start()

    loads[0].wait()
    turn_blocks(16, 0, FIRST // 128, send_a, 0)
    pl.semaphore_wait(barrier, DEV - 1)
    send_part(send_a, recv_a, send_sem.at[0], recv_sem_a.at[0], GROUP)
    loads[1].wait()
    loads[2].wait()

    for r in range(HALF):
        gap = jnp.zeros((128 - 2 * TAIL, 128), BF16)
        both = [xin[PAIRS + r, MAIN:NG, :], xin[PAIRS + HALF + r, MAIN:NG, :], gap]
        turn[1, :, r, :] = turned(jnp.concatenate(both, axis=0))
    send_t[...] = turn[1, :, :HALF, :].astype(BF16)
    send_part(send_t, recv_t, send_sem.at[2], recv_sem_a.at[2], GROUP)
    turn_blocks(16, FIRST // 128, 9, send_m, FIRST)
    send_part(send_m, recv_m, send_sem.at[1], recv_sem_a.at[1], GROUP)

    loads[3].wait()
    turn_blocks(0, 0, 9, own_main, 0)
    for r in range(PAIRS):
        gap = jnp.zeros((128 - 2 * TAIL, 128), BF16)
        both = [xin[r, MAIN:NG, :], xin[r, MAIN:NG, :], gap]
        turn[1, :, r, :] = turned(jnp.concatenate(both, axis=0))
    own_tail[...] = turn[1].astype(BF16)

    loads[4].wait()
    lane = lax.broadcasted_iota(jnp.int32, (TAIL, 128), 1)
    line = lax.broadcasted_iota(jnp.int32, (TAIL, 128), 0)
    twice = ((lane == line) | (lane == line + TAIL)).astype(F32).astype(BF16)
    w_wide[...] = jnp.zeros_like(w_wide)
    for row, first, count in ((0, MAIN, TAIL), (TAIL, MAIN, TAIL), (128, 0, MAIN)):
        w_wide[pl.ds(row, count), pl.ds(0, MAIN)] = w_in[pl.ds(first, count), pl.ds(0, MAIN)]
        ends = jnp.dot(w_in[pl.ds(first, count), pl.ds(MAIN, TAIL)], twice, preferred_element_type=F32)
        w_wide[pl.ds(row, count), pl.ds(MAIN, 128)] = ends.astype(BF16)
    spread[...] = same_block((ROWS, 256), 1, 16, 1, 16).astype(BF16)

    def pairing(slots):
        tall = lax.broadcasted_iota(jnp.int32, (slots * PAIRS, slots * HALF), 0)
        low = lax.broadcasted_iota(jnp.int32, (slots * PAIRS, slots * HALF), 1)
        pick = (tall // PAIRS == low // HALF) & (tall % HALF == low % HALF)
        b = lax.broadcasted_iota(jnp.int32, (slots * PAIRS, 128), 0) % PAIRS // HALF
        lane = lax.broadcasted_iota(jnp.int32, (slots * PAIRS, 128), 1) // TAIL
        return pick.astype(F32).astype(BF16), lane == b

    def apart(packed, slots):
        pick, held = pairing(slots)
        rows = jnp.dot(pick, packed, preferred_element_type=F32)
        return jnp.where(held, rows, 0.0).astype(BF16)

    def together(rows, slots):
        pick, held = pairing(slots)
        rows = jnp.where(held, rows, 0.0).astype(BF16)
        return lax.dot_general(pick, rows, (((0,), (0,)), ((), ())), preferred_element_type=F32).astype(BF16)

    nt = (((1,), (1,)), ((), ()))

    def screen(g, _):
        slots = pl.ds(g * GROUP, GROUP)
        for p, part in enumerate((recv_a, recv_m, recv_t)):
            view = part.at[slots]
            pltpu.make_async_copy(view, view, recv_sem_a.at[p, g]).wait()
        tail = apart(recv_t[slots].reshape(GROUP * HALF, 128), GROUP)
        main = jnp.concatenate([recv_a[slots], recv_m[slots]], axis=2).reshape(GROUP * PAIRS, MAIN)
        left = jnp.concatenate([main, tail], axis=1)
        ends = lax.dot_general(left, w_wide[pl.ds(0, 128), :], nt, preferred_element_type=F32)
        screened_t[slots] = together(ends, GROUP).reshape(GROUP, HALF, 128)

        def column(n, _):
            rows = pl.ds(pl.multiple_of(128 + n * 384, 128), 384)
            part = lax.dot_general(left, w_wide[rows, :], nt, preferred_element_type=F32)
            lanes = pl.ds(pl.multiple_of(n * 384, 128), 384)
            screened[slots, :, lanes] = part.astype(BF16).reshape(GROUP, PAIRS, 384)
            return 0

        lax.fori_loop(0, 3, column, 0)

        def pass_on(slot, _):
            to = from_ref[slot]
            for p, (src, dst) in enumerate(((screened, recv_s), (screened_t, recv_st))):
                pltpu.make_async_remote_copy(
                    src.at[slot], dst.at[slot], send_sem.at[3 + p], recv_sem_s.at[p, lax.div(slot, FEW)],
                    device_id=(to,), device_id_type=MESH,
                ).start()
            return 0

        @pl.when(g == 0)
        def _():
            for p, (src, dst) in enumerate(((screened, recv_s), (screened_t, recv_st))):
                pltpu.make_async_copy(src.at[0], dst.at[0], recv_sem_s.at[p, 0]).start()

        lax.fori_loop(jnp.where(g == 0, 1, g * GROUP), g * GROUP + GROUP, pass_on, 0)
        return 0

    lax.fori_loop(0, GROUPS, screen, 0)

    def contract(g, _):
        slots = pl.ds(g * FEW, FEW)
        places = [to_ref[g * FEW + i] for i in range(FEW)]
        mains = jnp.concatenate([own_main[q] for q in places], axis=0)
        tails = jnp.concatenate([own_tail[q] for q in places], axis=0)
        for p, part in enumerate((recv_s, recv_st)):
            view = part.at[slots]
            pltpu.make_async_copy(view, view, recv_sem_s.at[p, g]).wait()
        ends = apart(recv_st[slots].reshape(FEW * HALF, 128), FEW)
        every = lax.dot_general(mains, recv_s[slots].reshape(ROWS, MAIN), nt, preferred_element_type=F32)
        every = every + lax.dot_general(tails, ends, nt, preferred_element_type=F32)
        own = jnp.where(same_block((ROWS, ROWS), 16, 0, 16, 0), every, 0.0).astype(BF16)
        wide = jnp.dot(own, spread[...], preferred_element_type=F32)
        wide = jnp.where(same_block((ROWS, 256), 1, 16, 16, 0), wide, 0.0).astype(BF16)
        gather = same_block((FEW, ROWS), 1, FEW, 16, 0).astype(BF16)
        rows = jnp.dot(gather, wide, preferred_element_type=F32)
        for i, q in enumerate(places):
            landed[q, 0:1, :] = rows[i : i + 1, :128]
            landed[q, 1:2, :] = rows[i : i + 1, 128:]
        return 0

    loads[5].wait()
    ones = jnp.ones((DEV, 128), BF16)
    diagonal = jnp.where(same_block((DEV, DEV), 1, DEV, 1, DEV), live_ref[...].astype(F32), 0.0).astype(BF16)
    kept[...] = jnp.dot(diagonal, ones, preferred_element_type=F32)

    lax.fori_loop(0, FEWS, contract, 0)

    for p, part in enumerate((send_a, send_m, send_t, screened, screened_t)):
        view = part.at[pl.ds(1, DEV - 1)]
        pltpu.make_async_copy(view, view, send_sem.at[p]).wait()
    o_ref[:, :128] = (landed[:, 0, :] * kept[...]).astype(BF16)
    o_ref[:, 128:] = (landed[:, 1, :] * kept[...]).astype(BF16)


def on_device(densities, screening, live):
    x = jnp.transpose(densities, (1, 2, 3, 0))[0]
    blocks = pl.pallas_call(
        kernel,
        out_shape=jax.ShapeDtypeStruct((DEV, PAIRS * PAIRS), BF16),
        in_specs=[pl.BlockSpec(memory_space=pltpu.HBM)] * 3,
        out_specs=pl.BlockSpec(memory_space=pltpu.VMEM),
        scratch_shapes=[
            pltpu.VMEM((2 * PAIRS, NG, DEV), BF16),
            pltpu.VMEM((NG, NG), BF16),
            pltpu.VMEM((LANES_A, LANES_A), BF16),
            pltpu.VMEM((DEV, PAIRS, FIRST), BF16),
            pltpu.VMEM((DEV, PAIRS, REST), BF16),
            pltpu.VMEM((DEV, HALF, 128), BF16),
            pltpu.VMEM((DEV, PAIRS, FIRST), BF16),
            pltpu.VMEM((DEV, PAIRS, REST), BF16),
            pltpu.VMEM((DEV, HALF, 128), BF16),
            pltpu.VMEM((DEV, PAIRS, MAIN), BF16),
            pltpu.VMEM((DEV, PAIRS, 128), BF16),
            pltpu.VMEM((DEV, PAIRS, MAIN), BF16),
            pltpu.VMEM((DEV, HALF, 128), BF16),
            pltpu.VMEM((DEV, PAIRS, MAIN), BF16),
            pltpu.VMEM((DEV, HALF, 128), BF16),
            pltpu.VMEM((2, DEV, PAIRS, 128), F32),
            pltpu.VMEM((ROWS, 256), BF16),
            pltpu.VMEM((1, DEV), jnp.int32),
            pltpu.VMEM((DEV, 128), F32),
            pltpu.VMEM((DEV, 2, 128), F32),
            pltpu.SMEM((DEV,), jnp.int32),
            pltpu.SMEM((DEV,), jnp.int32),
            pltpu.SemaphoreType.DMA((6,)),
            pltpu.SemaphoreType.DMA((5,)),
            pltpu.SemaphoreType.DMA((3, GROUPS)),
            pltpu.SemaphoreType.DMA((2, FEWS)),
        ],
        compiler_params=pltpu.CompilerParams(
            collective_id=0, has_side_effects=True, vmem_limit_bytes=52 << 20
        ),
    )(x, screening[0], pltpu.with_memory_space_constraint(live.reshape(1, DEV), pltpu.HBM))
    return blocks[:, None, :]


def solution(mesh):
    in_specs = (P(None, "pb", None, None), P("pb", None, None), P(None, "pb"))
    return jax.shard_map(
        on_device, mesh=mesh, in_specs=in_specs, out_specs=P(None, "pb", None), check_vma=False
    )
```

```python
import jax
import jax.numpy as jnp
from jax import lax
from jax.experimental import pallas as pl
from jax.experimental.pallas import tpu as pltpu
from jax.sharding import PartitionSpec as P

F32 = jnp.float32
BF16 = jnp.bfloat16
MESH = pl.DeviceIdType.MESH

DEV = 128
PAIRS = 16
NG = 1200
MAIN = 1152
TAIL = NG - MAIN
LANES_A = MAIN + 128
HALF = PAIRS // 2
LANES_B = MAIN
STEP = 37
GROUP = 16
GROUPS = DEV // GROUP
FEW = 16
FEWS = DEV // FEW
ROWS = FEW * PAIRS
FIRST = 384
REST = MAIN - FIRST


def digits(i):
    return i // 32, i // 8 % 4, i // 2 % 4, i % 2


def hops(i):
    return sum(min(d, 4 - d) for d in digits(i)[:3])


_MIXED = [i * STEP % DEV for i in range(1, DEV)]
ORDER = [0] + sorted(_MIXED, key=lambda i: hops(i) <= 1)


def fill_places(me, to_ref, from_ref):
    z, x, y, c = lax.div(me, 32), lax.rem(lax.div(me, 8), 4), lax.rem(lax.div(me, 2), 4), lax.rem(me, 2)
    at = [
        [lax.rem(own + d, size) * unit for d in range(size)]
        for own, size, unit in ((z, 4, 32), (x, 4, 8), (y, 4, 2), (c, 2, 1))
    ]
    for slot, offset in enumerate(ORDER):
        there = digits(offset)
        back = [-d % size for d, size in zip(there, (4, 4, 4, 2))]
        to_ref[slot] = sum(column[d] for column, d in zip(at, there))
        from_ref[slot] = sum(column[d] for column, d in zip(at, back))


def same_block(shape, div0, mod0, div1, mod1):
    row = lax.broadcasted_iota(jnp.int32, shape, 0)
    col = lax.broadcasted_iota(jnp.int32, shape, 1)
    row = row // div0 if div0 > 1 else row % mod0
    col = col // div1 if div1 > 1 else col % mod1
    return row == col


def kernel(
    x_hbm, w_hbm, live_hbm, o_ref,
    xin, w_in, w_wide, send_a, send_m, send_t, recv_a, recv_m, recv_t, own_main, own_tail,
    screened, screened_t, recv_s, recv_st, turn, spread, same_q, same_a, gather, pick, held, live_ref, kept, landed,
    to_ref, from_ref, load_sem, send_sem, recv_sem_a, recv_sem_s,
):
    me = lax.axis_index("pb")

    loads = [
        pltpu.make_async_copy(x_hbm.at[pl.ds(16, 16), pl.ds(0, FIRST)], xin.at[pl.ds(16, 16), pl.ds(0, FIRST)], load_sem.at[0]),
        pltpu.make_async_copy(x_hbm.at[pl.ds(16, 16), pl.ds(FIRST, NG - FIRST)], xin.at[pl.ds(16, 16), pl.ds(FIRST, NG - FIRST)], load_sem.at[1]),
        pltpu.make_async_copy(x_hbm.at[pl.ds(0, 16), pl.ds(MAIN, TAIL)], xin.at[pl.ds(0, 16), pl.ds(MAIN, TAIL)], load_sem.at[2]),
        pltpu.make_async_copy(x_hbm.at[pl.ds(0, 16), pl.ds(0, MAIN)], xin.at[pl.ds(0, 16), pl.ds(0, MAIN)], load_sem.at[3]),
        pltpu.make_async_copy(w_hbm, w_in, load_sem.at[4]),
        pltpu.make_async_copy(live_hbm, live_ref, load_sem.at[5]),
    ]
    for load in loads:
        load.start()

    barrier = pltpu.get_barrier_semaphore()

    def greet(slot, _):
        pl.semaphore_signal(barrier, inc=1, device_id=(lax.rem(me + slot, DEV),), device_id_type=MESH)
        return 0

    for i in range(1, DEV):
        greet(i, 0)

    fill_places(me, to_ref, from_ref)

    def turned(block):
        return jnp.transpose(block).astype(F32)

    def turn_block(first_row, column, slot, out, out_column):
        for r in range(PAIRS):
            turn[slot, :, r, :] = turned(xin[first_row + r, pl.ds(column, 128), :])
        out[:, :, pl.ds(out_column, 128)] = turn[slot].astype(BF16)

    def turn_blocks(first_row, begin, end, out, left_out):
        def body(j, _):
            column = pl.multiple_of(j * 128, 128)
            turn_block(first_row, column, lax.rem(j, 2), out, pl.multiple_of(column - left_out, 128))
            return 0

        lax.fori_loop(begin, end, body, 0)

    def send_part(src, dst, sem_s, sem_r, group):

        def body(slot, _):
            to = to_ref[slot]
            pltpu.make_async_remote_copy(
                src.at[to], dst.at[slot], sem_s, sem_r.at[lax.div(slot, group)],
                device_id=(to,), device_id_type=MESH,
            ).start()
            return 0

        lax.fori_loop(1, DEV, body, 0)
        pltpu.make_async_copy(src.at[me], dst.at[0], sem_r.at[0]).start()

    loads[0].wait()
    turn_blocks(16, 0, FIRST // 128, send_a, 0)
    pl.semaphore_wait(barrier, DEV - 1)
    send_part(send_a, recv_a, send_sem.at[0], recv_sem_a.at[0], GROUP)
    loads[1].wait()
    loads[2].wait()

    for r in range(HALF):
        gap = jnp.zeros((128 - 2 * TAIL, 128), BF16)
        both = [xin[PAIRS + r, MAIN:NG, :], xin[PAIRS + HALF + r, MAIN:NG, :], gap]
        turn[1, :, r, :] = turned(jnp.concatenate(both, axis=0))
    send_t[...] = turn[1, :, :HALF, :].astype(BF16)
    send_part(send_t, recv_t, send_sem.at[2], recv_sem_a.at[2], GROUP)
    turn_blocks(16, FIRST // 128, 9, send_m, FIRST)
    send_part(send_m, recv_m, send_sem.at[1], recv_sem_a.at[1], GROUP)

    loads[3].wait()
    turn_blocks(0, 0, 9, own_main, 0)
    for r in range(PAIRS):
        gap = jnp.zeros((128 - 2 * TAIL, 128), BF16)
        both = [xin[r, MAIN:NG, :], xin[r, MAIN:NG, :], gap]
        turn[1, :, r, :] = turned(jnp.concatenate(both, axis=0))
    own_tail[...] = turn[1].astype(BF16)

    loads[4].wait()
    lane = lax.broadcasted_iota(jnp.int32, (TAIL, 128), 1)
    line = lax.broadcasted_iota(jnp.int32, (TAIL, 128), 0)
    twice = ((lane == line) | (lane == line + TAIL)).astype(F32).astype(BF16)
    w_wide[...] = jnp.zeros_like(w_wide)
    for row, first, count in ((0, MAIN, TAIL), (TAIL, MAIN, TAIL), (128, 0, MAIN)):
        w_wide[pl.ds(row, count), pl.ds(0, MAIN)] = w_in[pl.ds(first, count), pl.ds(0, MAIN)]
        ends = jnp.dot(w_in[pl.ds(first, count), pl.ds(MAIN, TAIL)], twice, preferred_element_type=F32)
        w_wide[pl.ds(row, count), pl.ds(MAIN, 128)] = ends.astype(BF16)
    spread[...] = same_block((ROWS, 256), 1, 16, 1, 16).astype(BF16)

    same_q[...] = same_block((ROWS, ROWS), 16, 0, 16, 0).astype(F32)
    same_a[...] = same_block((ROWS, 256), 1, 16, 16, 0).astype(F32)
    gather[...] = same_block((FEW, ROWS), 1, FEW, 16, 0).astype(BF16)
    tall = lax.broadcasted_iota(jnp.int32, (ROWS, FEW * HALF), 0)
    low = lax.broadcasted_iota(jnp.int32, (ROWS, FEW * HALF), 1)
    pick[...] = ((tall // PAIRS == low // HALF) & (tall % HALF == low % HALF)).astype(F32).astype(BF16)
    half = lax.broadcasted_iota(jnp.int32, (ROWS, 128), 0) % PAIRS // HALF
    held[...] = (lax.broadcasted_iota(jnp.int32, (ROWS, 128), 1) // TAIL == half).astype(F32)

    def apart(packed):
        rows = jnp.dot(pick[...], packed, preferred_element_type=F32)
        return (rows * held[...]).astype(BF16)

    def together(rows):
        rows = (rows * held[...]).astype(BF16)
        return lax.dot_general(pick[...], rows, (((0,), (0,)), ((), ())), preferred_element_type=F32).astype(BF16)

    nt = (((1,), (1,)), ((), ()))

    def screen(g, _):
        slots = pl.ds(g * GROUP, GROUP)
        for p, part in enumerate((recv_a, recv_m, recv_t)):
            view = part.at[slots]
            pltpu.make_async_copy(view, view, recv_sem_a.at[p, g]).wait()
        tail = apart(recv_t[slots].reshape(GROUP * HALF, 128))
        main = jnp.concatenate([recv_a[slots], recv_m[slots]], axis=2).reshape(GROUP * PAIRS, MAIN)
        left = jnp.concatenate([main, tail], axis=1)
        ends = lax.dot_general(left, w_wide[pl.ds(0, 128), :], nt, preferred_element_type=F32)
        screened_t[slots] = together(ends).reshape(GROUP, HALF, 128)

        def column(n, _):
            rows = pl.ds(pl.multiple_of(128 + n * 384, 128), 384)
            part = lax.dot_general(left, w_wide[rows, :], nt, preferred_element_type=F32)
            lanes = pl.ds(pl.multiple_of(n * 384, 128), 384)
            screened[slots, :, lanes] = part.astype(BF16).reshape(GROUP, PAIRS, 384)
            return 0

        lax.fori_loop(0, 3, column, 0)

        def pass_on(slot, _):
            to = from_ref[slot]
            for p, (src, dst) in enumerate(((screened, recv_s), (screened_t, recv_st))):
                pltpu.make_async_remote_copy(
                    src.at[slot], dst.at[slot], send_sem.at[3 + p], recv_sem_s.at[p, lax.div(slot, FEW)],
                    device_id=(to,), device_id_type=MESH,
                ).start()
            return 0

        @pl.when(g == 0)
        def _():
            for p, (src, dst) in enumerate(((screened, recv_s), (screened_t, recv_st))):
                pltpu.make_async_copy(src.at[0], dst.at[0], recv_sem_s.at[p, 0]).start()

        lax.fori_loop(jnp.where(g == 0, 1, g * GROUP), g * GROUP + GROUP, pass_on, 0)
        return 0

    lax.fori_loop(0, GROUPS, screen, 0)

    def contract(g, _):
        slots = pl.ds(g * FEW, FEW)
        places = [to_ref[g * FEW + i] for i in range(FEW)]
        mains = jnp.concatenate([own_main[q] for q in places], axis=0)
        tails = jnp.concatenate([own_tail[q] for q in places], axis=0)
        for p, part in enumerate((recv_s, recv_st)):
            view = part.at[slots]
            pltpu.make_async_copy(view, view, recv_sem_s.at[p, g]).wait()
        ends = apart(recv_st[slots].reshape(FEW * HALF, 128))
        every = lax.dot_general(mains, recv_s[slots].reshape(ROWS, MAIN), nt, preferred_element_type=F32)
        every = every + lax.dot_general(tails, ends, nt, preferred_element_type=F32)
        own = (every * same_q[...]).astype(BF16)
        wide = jnp.dot(own, spread[...], preferred_element_type=F32)
        wide = (wide * same_a[...]).astype(BF16)
        rows = jnp.dot(gather[...], wide, preferred_element_type=F32)
        for i, q in enumerate(places):
            landed[q, 0:1, :] = rows[i : i + 1, :128]
            landed[q, 1:2, :] = rows[i : i + 1, 128:]
        return 0

    loads[5].wait()
    ones = jnp.ones((DEV, 128), BF16)
    diagonal = jnp.where(same_block((DEV, DEV), 1, DEV, 1, DEV), live_ref[...].astype(F32), 0.0).astype(BF16)
    kept[...] = jnp.dot(diagonal, ones, preferred_element_type=F32)

    lax.fori_loop(0, FEWS, contract, 0)

    for p, part in enumerate((send_a, send_m, send_t, screened, screened_t)):
        view = part.at[pl.ds(1, DEV - 1)]
        pltpu.make_async_copy(view, view, send_sem.at[p]).wait()
    o_ref[:, :128] = (landed[:, 0, :] * kept[...]).astype(BF16)
    o_ref[:, 128:] = (landed[:, 1, :] * kept[...]).astype(BF16)


def on_device(densities, screening, live):
    x = jnp.transpose(densities, (1, 2, 3, 0))[0]
    blocks = pl.pallas_call(
        kernel,
        out_shape=jax.ShapeDtypeStruct((DEV, PAIRS * PAIRS), BF16),
        in_specs=[pl.BlockSpec(memory_space=pltpu.HBM)] * 3,
        out_specs=pl.BlockSpec(memory_space=pltpu.VMEM),
        scratch_shapes=[
            pltpu.VMEM((2 * PAIRS, NG, DEV), BF16),
            pltpu.VMEM((NG, NG), BF16),
            pltpu.VMEM((LANES_A, LANES_A), BF16),
            pltpu.VMEM((DEV, PAIRS, FIRST), BF16),
            pltpu.VMEM((DEV, PAIRS, REST), BF16),
            pltpu.VMEM((DEV, HALF, 128), BF16),
            pltpu.VMEM((DEV, PAIRS, FIRST), BF16),
            pltpu.VMEM((DEV, PAIRS, REST), BF16),
            pltpu.VMEM((DEV, HALF, 128), BF16),
            pltpu.VMEM((DEV, PAIRS, MAIN), BF16),
            pltpu.VMEM((DEV, PAIRS, 128), BF16),
            pltpu.VMEM((DEV, PAIRS, MAIN), BF16),
            pltpu.VMEM((DEV, HALF, 128), BF16),
            pltpu.VMEM((DEV, PAIRS, MAIN), BF16),
            pltpu.VMEM((DEV, HALF, 128), BF16),
            pltpu.VMEM((2, DEV, PAIRS, 128), F32),
            pltpu.VMEM((ROWS, 256), BF16),
            pltpu.VMEM((ROWS, ROWS), F32),
            pltpu.VMEM((ROWS, 256), F32),
            pltpu.VMEM((FEW, ROWS), BF16),
            pltpu.VMEM((ROWS, FEW * HALF), BF16),
            pltpu.VMEM((ROWS, 128), F32),
            pltpu.VMEM((1, DEV), jnp.int32),
            pltpu.VMEM((DEV, 128), F32),
            pltpu.VMEM((DEV, 2, 128), F32),
            pltpu.SMEM((DEV,), jnp.int32),
            pltpu.SMEM((DEV,), jnp.int32),
            pltpu.SemaphoreType.DMA((6,)),
            pltpu.SemaphoreType.DMA((5,)),
            pltpu.SemaphoreType.DMA((3, GROUPS)),
            pltpu.SemaphoreType.DMA((2, FEWS)),
        ],
        compiler_params=pltpu.CompilerParams(
            collective_id=0, has_side_effects=True, vmem_limit_bytes=52 << 20
        ),
    )(x, screening[0], pltpu.with_memory_space_constraint(live.reshape(1, DEV), pltpu.HBM))
    return blocks[:, None, :]


def solution(mesh):
    in_specs = (P(None, "pb", None, None), P("pb", None, None), P(None, "pb"))
    return jax.shard_map(
        on_device, mesh=mesh, in_specs=in_specs, out_specs=P(None, "pb", None), check_vma=False
    )
```

```python
import jax
import jax.numpy as jnp
from jax import lax
from jax.experimental import pallas as pl
from jax.experimental.pallas import tpu as pltpu
from jax.sharding import PartitionSpec as P

F32 = jnp.float32
BF16 = jnp.bfloat16
MESH = pl.DeviceIdType.MESH

DEV = 128
PAIRS = 16
NG = 1200
MAIN = 1152
TAIL = NG - MAIN
LANES_A = MAIN + 128
HALF = PAIRS // 2
LANES_B = MAIN
STEP = 37
GROUP = 16
GROUPS = DEV // GROUP
FEW = 16
FEWS = DEV // FEW
ROWS = FEW * PAIRS
FIRST = 384
REST = MAIN - FIRST


def digits(i):
    return i // 32, i // 8 % 4, i // 2 % 4, i % 2


def hops(i):
    return sum(min(d, 4 - d) for d in digits(i)[:3])


_MIXED = [i * STEP % DEV for i in range(1, DEV)]
ORDER = [0] + sorted(_MIXED, key=lambda i: hops(i) <= 1)


def fill_places(me, to_ref, from_ref):
    z, x, y, c = lax.div(me, 32), lax.rem(lax.div(me, 8), 4), lax.rem(lax.div(me, 2), 4), lax.rem(me, 2)
    at = [
        [lax.rem(own + d, size) * unit for d in range(size)]
        for own, size, unit in ((z, 4, 32), (x, 4, 8), (y, 4, 2), (c, 2, 1))
    ]
    for slot, offset in enumerate(ORDER):
        there = digits(offset)
        back = [-d % size for d, size in zip(there, (4, 4, 4, 2))]
        to_ref[slot] = sum(column[d] for column, d in zip(at, there))
        from_ref[slot] = sum(column[d] for column, d in zip(at, back))


def same_block(shape, div0, mod0, div1, mod1):
    row = lax.broadcasted_iota(jnp.int32, shape, 0)
    col = lax.broadcasted_iota(jnp.int32, shape, 1)
    row = row // div0 if div0 > 1 else row % mod0
    col = col // div1 if div1 > 1 else col % mod1
    return row == col


def kernel(
    x_hbm, w_hbm, live_hbm, o_ref,
    xin, w_in, w_wide, send_a, send_m, send_t, recv_a, recv_m, recv_t, own_main, own_tail,
    screened, screened_t, recv_s, recv_st, turn, spread, same_q, same_a, gather, pick, held, live_ref, kept, landed,
    to_ref, from_ref, load_sem, send_sem, recv_sem_a, recv_sem_s,
):
    me = lax.axis_index("pb")

    loads = [
        pltpu.make_async_copy(x_hbm.at[pl.ds(16, 16), pl.ds(0, FIRST)], xin.at[pl.ds(16, 16), pl.ds(0, FIRST)], load_sem.at[0]),
        pltpu.make_async_copy(x_hbm.at[pl.ds(16, 16), pl.ds(FIRST, NG - FIRST)], xin.at[pl.ds(16, 16), pl.ds(FIRST, NG - FIRST)], load_sem.at[1]),
        pltpu.make_async_copy(x_hbm.at[pl.ds(0, 16), pl.ds(MAIN, TAIL)], xin.at[pl.ds(0, 16), pl.ds(MAIN, TAIL)], load_sem.at[2]),
        pltpu.make_async_copy(x_hbm.at[pl.ds(0, 16), pl.ds(0, MAIN)], xin.at[pl.ds(0, 16), pl.ds(0, MAIN)], load_sem.at[3]),
        pltpu.make_async_copy(w_hbm, w_in, load_sem.at[4]),
        pltpu.make_async_copy(live_hbm, live_ref, load_sem.at[5]),
    ]
    for load in loads:
        load.start()

    barrier = pltpu.get_barrier_semaphore()

    def greet(slot, _):
        pl.semaphore_signal(barrier, inc=1, device_id=(lax.rem(me + slot, DEV),), device_id_type=MESH)
        return 0

    for i in range(1, DEV):
        greet(i, 0)

    fill_places(me, to_ref, from_ref)

    def turned(block):
        return jnp.transpose(block).astype(F32)

    def turn_block(first_row, column, slot, out, out_column):
        for r in range(PAIRS):
            turn[slot, :, r, :] = turned(xin[first_row + r, pl.ds(column, 128), :])
        out[:, :, pl.ds(out_column, 128)] = turn[slot].astype(BF16)

    def turn_blocks(first_row, begin, end, out, left_out):
        def body(j, _):
            column = pl.multiple_of(j * 128, 128)
            turn_block(first_row, column, lax.rem(j, 2), out, pl.multiple_of(column - left_out, 128))
            return 0

        lax.fori_loop(begin, end, body, 0)

    def send_part(src, dst, sem_s, sem_r, group):

        def body(slot, _):
            to = to_ref[slot]
            pltpu.make_async_remote_copy(
                src.at[to], dst.at[slot], sem_s, sem_r.at[lax.div(slot, group)],
                device_id=(to,), device_id_type=MESH,
            ).start()
            return 0

        lax.fori_loop(1, DEV, body, 0)
        pltpu.make_async_copy(src.at[me], dst.at[0], sem_r.at[0]).start()

    loads[0].wait()
    turn_blocks(16, 0, FIRST // 128, send_a, 0)
    pl.semaphore_wait(barrier, DEV - 1)
    send_part(send_a, recv_a, send_sem.at[0], recv_sem_a.at[0], GROUP)
    loads[1].wait()
    loads[2].wait()

    for r in range(HALF):
        gap = jnp.zeros((128 - 2 * TAIL, 128), BF16)
        both = [xin[PAIRS + r, MAIN:NG, :], xin[PAIRS + HALF + r, MAIN:NG, :], gap]
        turn[1, :, r, :] = turned(jnp.concatenate(both, axis=0))
    send_t[...] = turn[1, :, :HALF, :].astype(BF16)
    send_part(send_t, recv_t, send_sem.at[2], recv_sem_a.at[2], GROUP)
    turn_blocks(16, FIRST // 128, 9, send_m, FIRST)
    send_part(send_m, recv_m, send_sem.at[1], recv_sem_a.at[1], GROUP)

    loads[3].wait()
    turn_blocks(0, 0, 9, own_main, 0)
    for r in range(PAIRS):
        gap = jnp.zeros((128 - 2 * TAIL, 128), BF16)
        both = [xin[r, MAIN:NG, :], xin[r, MAIN:NG, :], gap]
        turn[1, :, r, :] = turned(jnp.concatenate(both, axis=0))
    own_tail[...] = turn[1].astype(BF16)

    loads[4].wait()
    lane = lax.broadcasted_iota(jnp.int32, (TAIL, 128), 1)
    line = lax.broadcasted_iota(jnp.int32, (TAIL, 128), 0)
    twice = ((lane == line) | (lane == line + TAIL)).astype(F32).astype(BF16)
    w_wide[...] = jnp.zeros_like(w_wide)
    for row, first, count in ((0, MAIN, TAIL), (TAIL, MAIN, TAIL), (128, 0, MAIN)):
        w_wide[pl.ds(row, count), pl.ds(0, MAIN)] = w_in[pl.ds(first, count), pl.ds(0, MAIN)]
        ends = jnp.dot(w_in[pl.ds(first, count), pl.ds(MAIN, TAIL)], twice, preferred_element_type=F32)
        w_wide[pl.ds(row, count), pl.ds(MAIN, 128)] = ends.astype(BF16)
    spread[...] = same_block((ROWS, 256), 1, 16, 1, 16).astype(BF16)

    same_q[...] = same_block((ROWS, ROWS), 16, 0, 16, 0).astype(F32)
    same_a[...] = same_block((ROWS, 256), 1, 16, 16, 0).astype(F32)
    gather[...] = same_block((FEW, ROWS), 1, FEW, 16, 0).astype(BF16)
    tall = lax.broadcasted_iota(jnp.int32, (ROWS, FEW * HALF), 0)
    low = lax.broadcasted_iota(jnp.int32, (ROWS, FEW * HALF), 1)
    pick[...] = ((tall // PAIRS == low // HALF) & (tall % HALF == low % HALF)).astype(F32).astype(BF16)
    half = lax.broadcasted_iota(jnp.int32, (ROWS, 128), 0) % PAIRS // HALF
    held[...] = (lax.broadcasted_iota(jnp.int32, (ROWS, 128), 1) // TAIL == half).astype(F32)

    def apart(packed):
        rows = jnp.dot(pick[...], packed, preferred_element_type=F32)
        return (rows * held[...]).astype(BF16)

    def together(rows):
        rows = (rows * held[...]).astype(BF16)
        return lax.dot_general(pick[...], rows, (((0,), (0,)), ((), ())), preferred_element_type=F32).astype(BF16)

    nt = (((1,), (1,)), ((), ()))

    def screen(g, _):
        slots = pl.ds(g * GROUP, GROUP)
        for p, part in enumerate((recv_a, recv_m, recv_t)):
            view = part.at[slots]
            pltpu.make_async_copy(view, view, recv_sem_a.at[p, g]).wait()
        tail = apart(recv_t[slots].reshape(GROUP * HALF, 128))
        main = jnp.concatenate([recv_a[slots], recv_m[slots]], axis=2).reshape(GROUP * PAIRS, MAIN)
        left = jnp.concatenate([main, tail], axis=1)
        ends = lax.dot_general(left, w_wide[pl.ds(0, 128), :], nt, preferred_element_type=F32)
        screened_t[slots] = together(ends).reshape(GROUP, HALF, 128)

        def column(n, _):
            rows = pl.ds(pl.multiple_of(128 + n * 384, 128), 384)
            part = lax.dot_general(left, w_wide[rows, :], nt, preferred_element_type=F32)
            lanes = pl.ds(pl.multiple_of(n * 384, 128), 384)
            screened[slots, :, lanes] = part.astype(BF16).reshape(GROUP, PAIRS, 384)
            return 0

        lax.fori_loop(0, 3, column, 0)

        def pass_on(slot, _):
            to = from_ref[slot]
            for p, (src, dst) in ((1, (screened_t, recv_st)), (0, (screened, recv_s))):
                pltpu.make_async_remote_copy(
                    src.at[slot], dst.at[slot], send_sem.at[3 + p], recv_sem_s.at[p, lax.div(slot, FEW)],
                    device_id=(to,), device_id_type=MESH,
                ).start()
            return 0

        @pl.when(g == 0)
        def _():
            for p, (src, dst) in enumerate(((screened, recv_s), (screened_t, recv_st))):
                pltpu.make_async_copy(src.at[0], dst.at[0], recv_sem_s.at[p, 0]).start()

        lax.fori_loop(jnp.where(g == 0, 1, g * GROUP), g * GROUP + GROUP, pass_on, 0)
        return 0

    lax.fori_loop(0, GROUPS, screen, 0)

    def contract(g, _):
        slots = pl.ds(g * FEW, FEW)
        places = [to_ref[g * FEW + i] for i in range(FEW)]
        mains = jnp.concatenate([own_main[q] for q in places], axis=0)
        tails = jnp.concatenate([own_tail[q] for q in places], axis=0)
        view = recv_st.at[slots]
        pltpu.make_async_copy(view, view, recv_sem_s.at[1, g]).wait()
        ends = apart(recv_st[slots].reshape(FEW * HALF, 128))
        early = lax.dot_general(tails, ends, nt, preferred_element_type=F32)
        view = recv_s.at[slots]
        pltpu.make_async_copy(view, view, recv_sem_s.at[0, g]).wait()
        every = early + lax.dot_general(mains, recv_s[slots].reshape(ROWS, MAIN), nt, preferred_element_type=F32)
        own = (every * same_q[...]).astype(BF16)
        wide = jnp.dot(own, spread[...], preferred_element_type=F32)
        wide = (wide * same_a[...]).astype(BF16)
        rows = jnp.dot(gather[...], wide, preferred_element_type=F32)
        for i, q in enumerate(places):
            landed[q, 0:1, :] = rows[i : i + 1, :128]
            landed[q, 1:2, :] = rows[i : i + 1, 128:]
        return 0

    loads[5].wait()
    ones = jnp.ones((DEV, 128), BF16)
    diagonal = jnp.where(same_block((DEV, DEV), 1, DEV, 1, DEV), live_ref[...].astype(F32), 0.0).astype(BF16)
    kept[...] = jnp.dot(diagonal, ones, preferred_element_type=F32)

    lax.fori_loop(0, FEWS, contract, 0)

    for p, part in enumerate((send_a, send_m, send_t, screened, screened_t)):
        view = part.at[pl.ds(1, DEV - 1)]
        pltpu.make_async_copy(view, view, send_sem.at[p]).wait()
    o_ref[:, :128] = (landed[:, 0, :] * kept[...]).astype(BF16)
    o_ref[:, 128:] = (landed[:, 1, :] * kept[...]).astype(BF16)


def on_device(densities, screening, live):
    x = jnp.transpose(densities, (1, 2, 3, 0))[0]
    blocks = pl.pallas_call(
        kernel,
        out_shape=jax.ShapeDtypeStruct((DEV, PAIRS * PAIRS), BF16),
        in_specs=[pl.BlockSpec(memory_space=pltpu.HBM)] * 3,
        out_specs=pl.BlockSpec(memory_space=pltpu.VMEM),
        scratch_shapes=[
            pltpu.VMEM((2 * PAIRS, NG, DEV), BF16),
            pltpu.VMEM((NG, NG), BF16),
            pltpu.VMEM((LANES_A, LANES_A), BF16),
            pltpu.VMEM((DEV, PAIRS, FIRST), BF16),
            pltpu.VMEM((DEV, PAIRS, REST), BF16),
            pltpu.VMEM((DEV, HALF, 128), BF16),
            pltpu.VMEM((DEV, PAIRS, FIRST), BF16),
            pltpu.VMEM((DEV, PAIRS, REST), BF16),
            pltpu.VMEM((DEV, HALF, 128), BF16),
            pltpu.VMEM((DEV, PAIRS, MAIN), BF16),
            pltpu.VMEM((DEV, PAIRS, 128), BF16),
            pltpu.VMEM((DEV, PAIRS, MAIN), BF16),
            pltpu.VMEM((DEV, HALF, 128), BF16),
            pltpu.VMEM((DEV, PAIRS, MAIN), BF16),
            pltpu.VMEM((DEV, HALF, 128), BF16),
            pltpu.VMEM((2, DEV, PAIRS, 128), F32),
            pltpu.VMEM((ROWS, 256), BF16),
            pltpu.VMEM((ROWS, ROWS), F32),
            pltpu.VMEM((ROWS, 256), F32),
            pltpu.VMEM((FEW, ROWS), BF16),
            pltpu.VMEM((ROWS, FEW * HALF), BF16),
            pltpu.VMEM((ROWS, 128), F32),
            pltpu.VMEM((1, DEV), jnp.int32),
            pltpu.VMEM((DEV, 128), F32),
            pltpu.VMEM((DEV, 2, 128), F32),
            pltpu.SMEM((DEV,), jnp.int32),
            pltpu.SMEM((DEV,), jnp.int32),
            pltpu.SemaphoreType.DMA((6,)),
            pltpu.SemaphoreType.DMA((5,)),
            pltpu.SemaphoreType.DMA((3, GROUPS)),
            pltpu.SemaphoreType.DMA((2, FEWS)),
        ],
        compiler_params=pltpu.CompilerParams(
            collective_id=0, has_side_effects=True, vmem_limit_bytes=52 << 20
        ),
    )(x, screening[0], pltpu.with_memory_space_constraint(live.reshape(1, DEV), pltpu.HBM))
    return blocks[:, None, :]


def solution(mesh):
    in_specs = (P(None, "pb", None, None), P("pb", None, None), P(None, "pb"))
    return jax.shard_map(
        on_device, mesh=mesh, in_specs=in_specs, out_specs=P(None, "pb", None), check_vma=False
    )
```
